256 devices in a mesh: date: 64 (over x_hi, y, z), strip: 4 (over x_lo, core).
Axes of the slice: x: 4 (x_hi: 2, x_lo: 2; x = x_hi * 2 + x_lo), y: 4, z: 8, core: 2. Of those that a mesh axis runs over, the one named last changes fastest.
Arguments:
- scenes: bfloat16 [2, 128, 128, 4096], P(None, 'date', 'strip'), may hold values from -6 to 6
- date_pairs: int32 [96, 2], replicated, may hold values from 0 to 127, as said below
- first_weight: bfloat16 [3, 3, 64, 2], replicated, may hold values from -4 to 4
- mid_weight: bfloat16 [2, 3, 3, 64, 64], replicated, may hold values from -0.375 to 0.375
- last_weight: bfloat16 [3, 3, 1, 64], replicated, may hold values from -0.375 to 0.375
- inversion: float32 [128, 96], replicated, may hold values from -0.625 to 0.625
Outputs:
- displacement: float32 [128, 32, 256], P('date', 'strip')
The draws below stay inside these ranges and needn't reach their ends.
Inputs may be any that keep to these rules, and one draw needn't show every extreme that they name: `date_pairs`: Write g(d) = d // 2 for the date group of date d; in matching m, g of the reference date and g of the secondary date differ exactly in the bit of value step, and every group in 0..2 32 - 1 appears in exactly one interferogram of each matching. Which side is the reference and which date of a group is used vary.
All inputs are finite; a program needn't handle non-finite values.
Results may differ from the reference program's by a relative error of at most 0.02.
Values may be sent and summed in bfloat16 or wider, within the bound.
No kernel may reach another device: no remote copies, remote signals or barrier semaphores. Data moves between devices by JAX's collectives and lax.ppermute only.
A program may use at most 64 MiB of HBM per device.

```python
import jax
import jax.numpy as jnp
import numpy as np
from jax import lax

COLS = 4096
DATE_DEV = 2
CH = 64
MIDS = 2
LOOK_R = 4
LOOK_C = 16
DEV_HALF = 32
DATES = 128
PAIRS = 96
ROWS = 128


def draw_date_pairs(key, part):
    total_groups = 2 * DEV_HALF
    bit_list = [0, 1, DEV_HALF.bit_length() - 1]
    blocks = []
    for which in range(3):
        bit_pos = bit_list[which]
        lower_groups = np.array([group for group in range(total_groups) if not group >> bit_pos & 1], np.int32)
        key_order, key_side, key_local = jax.random.split(jax.random.fold_in(key, which + 11), 3)
        shuffled = jax.random.permutation(key_order, jnp.asarray(lower_groups))
        upper_groups = shuffled + (1 << bit_pos)
        flipped = jax.random.randint(key_side, (DEV_HALF,), 0, 2)
        local_dates = jax.random.randint(key_local, (DEV_HALF, 2), 0, DATE_DEV)
        ref_group = jnp.where(flipped == 1, upper_groups, shuffled)
        sec_group = jnp.where(flipped == 1, shuffled, upper_groups)
        ref_date = ref_group * DATE_DEV + local_dates[:, 0]
        sec_date = sec_group * DATE_DEV + local_dates[:, 1]
        blocks.append(jnp.stack([ref_date, sec_date], axis=1))
    return jnp.concatenate(blocks, axis=0).astype(jnp.int32)


def block_levels(rng, dims, pieces, least, top_value):
    gain = 1.0
    for dim, parts in pieces:
        heights = jax.random.uniform(jax.random.fold_in(jax.random.fold_in(rng, 6), dim), (parts,), jnp.float32, least / len(pieces), top_value / len(pieces))
        gain = gain * jnp.repeat(jnp.exp(heights), dims[dim] // parts).reshape((-1,) + (1,) * (len(dims) - 1 - dim))
    return gain


def noise(stream_key, shape, width, bound, cuts=(), dtype=jnp.bfloat16):
    values = width * jax.random.normal(stream_key, shape, jnp.float32)
    if cuts:
        values = values * block_levels(stream_key, shape, cuts, -0.22, 0.18)
    return jnp.clip(values, -bound, bound).astype(dtype)


def setup_inputs(seed: int = 0) -> dict:
    splits = jax.random.split(jax.random.key(seed), 7)
    scenes = noise(splits[0], (2, DATES, ROWS, COLS), 1.0, 6.0, ((1, 64), (2, 4)))
    date_pairs = draw_date_pairs(jax.random.fold_in(splits[6], 71), 0)
    first_weight = noise(splits[2], (3, 3, CH, 2), 2 ** -0.5, 4.0)
    mid_weight = noise(splits[3], (MIDS, 3, 3, CH, CH), (9 * CH // 2) ** -0.5, 0.375)
    last_weight = noise(splits[4], (3, 3, 1, CH), (9 * CH // 2) ** -0.5, 0.375)
    inversion = noise(splits[5], (DATES, PAIRS), PAIRS ** -0.5, 0.625, (), jnp.float32)
    return {"scenes": scenes, "date_pairs": date_pairs, "first_weight": first_weight, "mid_weight": mid_weight, "last_weight": last_weight, "inversion": inversion}


def look_sum(field):
    lead = field.shape[:-2]
    count_rows = field.shape[-2]
    count_cols = field.shape[-1]
    shaped = field.reshape(lead + (count_rows // LOOK_R, LOOK_R, count_cols // LOOK_C, LOOK_C))
    return shaped.sum(axis=(-3, -1))

def coherence_of(first, second):
    first = first.astype(jnp.float32)
    second = second.astype(jnp.float32)
    real_part = first[0] * second[0] + first[1] * second[1]
    imag_part = first[1] * second[0] - first[0] * second[1]
    first_power = first[0] * first[0] + first[1] * first[1]
    second_power = second[0] * second[0] + second[1] * second[1]
    scale = lax.rsqrt(look_sum(first_power) * look_sum(second_power) + 1e-06)
    return (jnp.stack([look_sum(real_part), look_sum(imag_part)]) * scale).astype(jnp.bfloat16)

def convolve(field, weight):
    padded = jnp.pad(field.astype(jnp.float32), ((0, 0), (1, 1), (1, 1)))
    count_rows = field.shape[1]
    count_cols = field.shape[2]
    weight = weight.astype(jnp.float32)
    total = jnp.zeros((weight.shape[2], count_rows, count_cols), jnp.float32)
    for tap_row in range(3):
        for tap_col in range(3):
            piece = padded[:, tap_row:tap_row + count_rows, tap_col:tap_col + count_cols]
            total = total + jnp.einsum('oi,irc->orc', weight[tap_row, tap_col], piece)
    return total

def one_pair(scenes, first_weight, mid_weight, last_weight, pair_row):
    first = lax.dynamic_index_in_dim(scenes, pair_row[0], 1, keepdims=False)
    second = lax.dynamic_index_in_dim(scenes, pair_row[1], 1, keepdims=False)
    hidden = coherence_of(first, second)
    hidden = jax.nn.relu(convolve(hidden, first_weight)).astype(jnp.bfloat16)
    for inner in range(MIDS):
        hidden = jax.nn.relu(convolve(hidden, mid_weight[inner])).astype(jnp.bfloat16)
    return convolve(hidden, last_weight)[0].astype(jnp.bfloat16)

def reference(scenes, date_pairs, first_weight, mid_weight, last_weight, inversion):
    phases = lax.map(lambda pair_row: one_pair(scenes, first_weight, mid_weight, last_weight, pair_row), date_pairs)
    return jnp.einsum('dk,krc->drc', inversion, phases.astype(jnp.float32), precision=lax.Precision.HIGHEST)
```

```python
import functools

import jax
import jax.numpy as jnp
import numpy as np
from jax import lax
from jax.experimental import pallas as pl
from jax.experimental.pallas import tpu as pltpu
from jax.sharding import PartitionSpec as P

BF = jnp.bfloat16
F32 = jnp.float32
LOOK_R = 4
LOOK_C = 16
HALO = 4
PITCH = 144
PIECE_COLS = 136
STRIP_ROWS = 8
FLAT = STRIP_ROWS * PITCH
EXT = (STRIP_ROWS + 2 * HALO) * PITCH
BITS = (0, 1, 5)
ORDER = (1, 2, 0)
SMEM = pltpu.SMEM
VMEM = pltpu.VMEM


def spec(space):
    return pl.BlockSpec(memory_space=space)


def prep_kernel(me_ref, pairs_ref, scenes_ref, send0, send1, send2, info_ref, sems):
    me = me_ref[0]
    sends = (send0, send1, send2)
    block = pairs_ref.shape[0] // 3
    width = send0.shape[2]
    total = scenes_ref.shape[3]
    copies = []
    for which in ORDER:

        def step(slot, carry):
            date, is_ref = carry
            first = pairs_ref[which * block + slot, 0]
            second = pairs_ref[which * block + slot, 1]
            hit_first = (first >> 1) == me
            hit_second = (second >> 1) == me
            date = jnp.where(hit_first, first, jnp.where(hit_second, second, date))
            return date, jnp.where(hit_first, 1, is_ref)

        date, is_ref = lax.fori_loop(0, block, step, (0, 0), unroll=True)
        local = jnp.clip(date - 2 * me, 0, 1)
        is_upper = (me >> BITS[which]) & 1
        info_ref[2 * which] = local
        info_ref[2 * which + 1] = is_ref
        start = pl.multiple_of((1 - is_upper) * (total - width), 128)
        copy = pltpu.make_async_copy(
            scenes_ref.at[:, local, :, pl.ds(start, width)], sends[which], sems.at[which]
        )
        copy.start()
        copies.append(copy)
    for copy in copies:
        copy.wait()


def coef_kernel(pairs_ref, rows_ref, coef_ref):
    block = pairs_ref.shape[0] // 3
    groups = 2 * block
    for which in range(3):

        def step(slot, carry):
            pair = which * block + slot
            first = pairs_ref[pair, 0] >> 1
            second = pairs_ref[pair, 1] >> 1
            for date in range(2):
                value = rows_ref[date, pair]
                base = (which * 2 + date) * groups
                coef_ref[base + first] = value
                coef_ref[base + second] = value
            return carry

        lax.fori_loop(0, block, step, 0, unroll=8)


def coherence_kernel(
    me_ref, info_ref, scenes_ref, recv0, recv1, recv2, out_ref, own, flat, sems
):
    me = me_ref[0]
    recvs = (recv0, recv1, recv2)
    width = recv0.shape[2]
    total = scenes_ref.shape[3]
    copies = {}
    for which in ORDER:
        is_upper = (me >> BITS[which]) & 1
        start = pl.multiple_of(is_upper * (total - width), 128)
        copies[which] = pltpu.make_async_copy(
            scenes_ref.at[:, info_ref[2 * which], :, pl.ds(start, width)],
            own.at[which],
            sems.at[which],
        )
        copies[which].start()
    lane = lax.broadcasted_iota(jnp.int32, (256, 128), 0)
    column = lax.broadcasted_iota(jnp.int32, (256, 128), 1)
    pool = jnp.where((lane & 127) >> 4 == column, 1.0, 0.0).astype(BF)
    flat[...] = jnp.zeros_like(flat)
    tiles = width // 128
    for which in ORDER:
        copies[which].wait()
        acc0 = None
        acc1 = None
        for tile in range(tiles):
            cols = slice(tile * 128, tile * 128 + 128)
            a0 = own[which, 0, :, cols].astype(F32)
            a1 = own[which, 1, :, cols].astype(F32)
            b0 = recvs[which][0, :, cols].astype(F32)
            b1 = recvs[which][1, :, cols].astype(F32)
            terms = jnp.concatenate(
                [a0 * b0 + a1 * b1, a1 * b0 - a0 * b1, a0 * a0 + a1 * a1, b0 * b0 + b1 * b1],
                axis=0,
            )
            high = terms.astype(BF)
            low = (terms - high.astype(F32)).astype(BF)
            part = jnp.dot(
                jnp.concatenate([high, low], axis=1), pool, preferred_element_type=F32
            )
            if tile == 0:
                acc0 = part
            elif tile < 16:
                acc0 = acc0 + pltpu.roll(part, 8 * tile, 1)
            else:
                acc1 = part
        sign = jnp.where(info_ref[2 * which + 1] == 1, 1.0, -1.0).astype(F32)
        for left, acc in ((0, acc0), (128, acc1)):
            grouped = acc.reshape(16, 8, 128)
            grouped = grouped + pltpu.roll(grouped, 7, 1)
            grouped = grouped + pltpu.roll(grouped, 6, 1)
            real, imag, power_a, power_b = (grouped[4 * i : 4 * i + 4] for i in range(4))
            scale = lax.rsqrt(power_a * power_b + 1e-06)
            real = real * scale
            imag = imag * (scale * sign)
            size = min(128, PITCH - left)
            for row in range(STRIP_ROWS):
                at = row * PITCH + left
                sub = 4 * (row % 2)
                for channel, value in ((0, real), (1, imag)):
                    slot = 2 * which + channel
                    flat[slot : slot + 1, at : at + size] = value[
                        row // 2, sub : sub + 1, :size
                    ]
    out_ref[...] = flat[...].astype(BF)


def conv_kernel(
    me_ref, strip_ref, own_ref, up_ref, down_ref, place_ref, w1_ref, w2_ref, w4_ref,
    out_ref, xs, taps, hidden_a, hidden_b, zs, mask_ref, phases
):
    me = me_ref[0]
    strip = strip_ref[0]
    strips = strip_ref[1]
    edge = HALO * PITCH
    row = place_ref[...] + (strip * STRIP_ROWS).astype(F32)
    limit = (strips * STRIP_ROWS).astype(F32)
    mask_ref[...] = jnp.where((row >= 0.0) & (row < limit), 1.0, 0.0).astype(F32)
    xs[:, 0:edge] = up_ref[:, FLAT - edge : FLAT].astype(F32)
    xs[:, edge : edge + FLAT] = own_ref[...].astype(F32)
    xs[:, edge + FLAT : EXT] = down_ref[:, 0:edge].astype(F32)
    x = xs[...] * mask_ref[...]
    for p in range(3):
        for q in range(3):
            shift = (p - 1) * PITCH + q - 1
            k = 3 * p + q
            moved = x if shift == 0 else pltpu.roll(x, (-shift) % EXT, 1)
            taps[8 * k : 8 * k + 8, :] = moved.astype(BF)
    hidden_a[...] = jnp.zeros_like(hidden_a)
    hidden_b[...] = jnp.zeros_like(hidden_b)

    def masked(value, lo, hi):
        rows = value.shape[0]
        value = jnp.maximum(value, 0.0).reshape(rows // 8, 8, hi - lo)
        value = value * mask_ref[:, lo:hi][None]
        return value.reshape(rows, hi - lo).astype(BF)

    def layer(source, weight, lo, hi):
        stacked = jnp.concatenate(
            [
                source[:, lo - PITCH : hi - PITCH],
                source[:, lo:hi],
                source[:, lo + PITCH : hi + PITCH],
            ],
            axis=0,
        )
        return jnp.dot(weight, stacked, preferred_element_type=F32)

    def across(parts, rows, size):
        left, mid, right = parts[0:rows], parts[rows : 2 * rows], parts[2 * rows : 3 * rows]
        return pltpu.roll(left, 1, 1) + mid + pltpu.roll(right, size - 1, 1)

    for which in range(3):
        lo, hi = 128, 2176
        value = jnp.dot(w1_ref[which], taps[:, lo:hi], preferred_element_type=F32)
        hidden_a[:, lo:hi] = masked(value, lo, hi)
        lo, hi = 256, 2048
        value = across(layer(hidden_a, w2_ref[0], lo, hi), 64, hi - lo)
        hidden_b[:, lo:hi] = masked(value, lo, hi)
        lo, hi = 384, 1920
        value = across(layer(hidden_b, w2_ref[1], lo, hi), 64, hi - lo)
        hidden_three = masked(value, lo, hi)
        value = jnp.dot(w4_ref[...], hidden_three, preferred_element_type=F32)
        zs[...] = across(value, 8, hi - lo)
        is_upper = (me >> BITS[which]) & 1
        for r in range(STRIP_ROWS):
            at = (r + HALO) * PITCH - lo
            halves = []
            for move in (0, 8):
                start = at + move
                halves.append(
                    zs[0:1, start - PITCH : start - PITCH + 128]
                    + zs[1:2, start : start + 128]
                    + zs[2:3, start + PITCH : start + PITCH + 128]
                )
            phases[r : r + 1, :] = jnp.where(is_upper == 1, halves[1], halves[0])
        phase = phases[...].astype(BF)
        for target in range(out_ref.shape[0]):
            out_ref[target, which] = phase


def sum_kernel(coef_ref, gathered_ref, out_ref):
    groups = gathered_ref.shape[0]
    acc = [[jnp.zeros((8, 128), F32) for _ in range(2)] for _ in range(2)]
    for group in range(groups):
        for which in range(3):
            side = group >> BITS[which] & 1
            phase = gathered_ref[group, which].astype(F32)
            for date in range(2):
                coef = coef_ref[(which * 2 + date) * groups + group]
                acc[date][side] = acc[date][side] + coef * phase
    for date in range(2):
        for side in range(2):
            out_ref[date, :, side * 128 : side * 128 + 128] = acc[date][side]


def place_of():
    lane = np.arange(EXT)
    row = np.where(lane % PITCH < PIECE_COLS, lane // PITCH - HALO, -1000)
    return np.broadcast_to(row.astype(np.float32), (8, EXT))


def per_device(scenes, date_pairs, first_weight, mid_weight, last_weight, inversion):
    groups = lax.axis_size("date")
    strips = lax.axis_size("strip")
    me = lax.axis_index("date").astype(jnp.int32)
    strip = lax.axis_index("strip").astype(jnp.int32)
    me_arr = me[None]
    strip_arr = jnp.stack([strip, jnp.int32(strips)])
    width = PIECE_COLS * LOOK_C
    rows = scenes.shape[2]
    ch = first_weight.shape[2]

    piece = jax.ShapeDtypeStruct((2, rows, width), BF)
    *sends, info = pl.pallas_call(
        prep_kernel,
        name="prep",
        out_shape=[piece] * 3 + [jax.ShapeDtypeStruct((8,), jnp.int32)],
        in_specs=[spec(SMEM), spec(SMEM), spec(pl.ANY)],
        out_specs=[spec(VMEM)] * 3 + [spec(SMEM)],
        scratch_shapes=[pltpu.SemaphoreType.DMA((3,))],
    )(me_arr, date_pairs, scenes)

    recvs = [None] * 3
    for which in ORDER:
        route = [(low, low ^ 1 << BITS[which]) for low in range(groups)]
        recvs[which] = lax.ppermute(sends[which], "date", route)

    own_rows = lax.dynamic_slice_in_dim(inversion, 2 * me, 2, axis=0)
    coef = pl.pallas_call(
        coef_kernel,
        name="coef",
        out_shape=jax.ShapeDtypeStruct((6 * groups,), F32),
        in_specs=[spec(SMEM), spec(SMEM)],
        out_specs=spec(SMEM),
        cost_estimate=pl.CostEstimate(flops=2000000, bytes_accessed=4000000, transcendentals=0),
    )(date_pairs, own_rows)

    looked = pl.pallas_call(
        coherence_kernel,
        name="coherence",
        out_shape=jax.ShapeDtypeStruct((8, FLAT), BF),
        in_specs=[spec(SMEM), spec(SMEM), spec(pl.ANY)] + [spec(VMEM)] * 3,
        out_specs=spec(VMEM),
        scratch_shapes=[
            pltpu.VMEM((3, 2, rows, width), BF),
            pltpu.VMEM((8, FLAT), F32),
            pltpu.SemaphoreType.DMA((3,)),
        ],
    )(me_arr, info, scenes, *recvs)

    up = lax.ppermute(looked, "strip", [(i, (i + 1) % strips) for i in range(strips)])
    down = lax.ppermute(looked, "strip", [((i + 1) % strips, i) for i in range(strips)])

    w1 = jnp.transpose(first_weight, (2, 0, 1, 3)).reshape(ch, 9, 2)
    w1 = jnp.stack(
        [jnp.pad(w1, ((0, 0), (0, 0), (2 * m, 6 - 2 * m))).reshape(ch, 72) for m in range(3)]
    )
    w2 = jnp.transpose(mid_weight, (0, 2, 3, 1, 4)).reshape(2, 3 * ch, 3 * ch)
    w4 = jnp.transpose(last_weight[:, :, 0], (1, 0, 2))
    w4 = jnp.pad(w4, ((0, 0), (0, 5), (0, 0))).reshape(24, ch)

    phases = pl.pallas_call(
        conv_kernel,
        name="convs",
        out_shape=jax.ShapeDtypeStruct((groups, 3, STRIP_ROWS, 128), BF),
        in_specs=[spec(SMEM)] * 2 + [spec(VMEM)] * 7,
        out_specs=spec(VMEM),
        scratch_shapes=[
            pltpu.VMEM((8, EXT), F32),
            pltpu.VMEM((72, EXT), BF),
            pltpu.VMEM((ch, EXT), BF),
            pltpu.VMEM((ch, EXT), BF),
            pltpu.VMEM((8, 1536), F32),
            pltpu.VMEM((8, EXT), F32),
            pltpu.VMEM((8, 128), F32),
        ],
    )(me_arr, strip_arr, looked, up, down, jnp.asarray(place_of()), w1, w2, w4)

    gathered = lax.all_to_all(phases, "date", 0, 0, tiled=True)

    return pl.pallas_call(
        sum_kernel,
        name="sums",
        out_shape=jax.ShapeDtypeStruct((2, STRIP_ROWS, 256), F32),
        in_specs=[spec(SMEM), spec(VMEM)],
        out_specs=spec(VMEM),
    )(coef, gathered)


def solution(mesh):
    return jax.shard_map(
        per_device,
        mesh=mesh,
        in_specs=(P(None, "date", "strip", None), P(), P(), P(), P(), P()),
        out_specs=P("date", "strip", None),
        check_vma=False,
    )
```

```python
import functools

import jax
import jax.numpy as jnp
from jax import lax
from jax.experimental import pallas as pl
from jax.experimental.pallas import tpu as pltpu
from jax.sharding import PartitionSpec as P


BF = jnp.bfloat16
F32 = jnp.float32
LOOK_C = 16
HALO = 4
PITCH = 144
PIECE_COLS = 136
STRIP_ROWS = 8
FLAT = STRIP_ROWS * PITCH
EXT = (STRIP_ROWS + 2 * HALO) * PITCH
BITS = (0, 1, 5)
SWAPS = (2, 1, 0)
GROUPS = ((2,), (0,), (1,))
PART = 8 * PITCH
SMEM = pltpu.SMEM
VMEM = pltpu.VMEM


def in_vmem(x):
    return pltpu.with_memory_space_constraint(x, pltpu.VMEM)


def spec(space):
    return pl.BlockSpec(memory_space=space)


def prep_kernel(pairs_ref, scenes_ref, *refs):
    *sends, info_ref, sems = refs
    me = lax.axis_index("date")
    both = pairs_ref[...]
    block = both.shape[1] // 3
    lane = lax.broadcasted_iota(jnp.int32, both.shape, 1)
    side = lax.broadcasted_iota(jnp.int32, both.shape, 0)
    code = (both & 1) + jnp.where(side == 0, 2, 0)
    weight = jnp.where(lane < block, 1, jnp.where(lane < 2 * block, 4, 16))
    code = jnp.where((both >> 1) == me, code * weight, 0).astype(F32)
    packed = jnp.sum(code).astype(jnp.int32)
    width = sends[0].shape[2]
    total = scenes_ref.shape[3]
    copies = []
    for slot, which in enumerate(SWAPS):
        local = (packed >> (2 * which)) & 1
        is_upper = (me >> BITS[which]) & 1
        start = pl.multiple_of((1 - is_upper) * (total - width), 128)
        copy = pltpu.make_async_copy(
            scenes_ref.at[:, local, :, pl.ds(start, width)], sends[slot], sems.at[slot]
        )
        copy.start()
        copies.append(copy)
        info_ref[2 * which] = local
        info_ref[2 * which + 1] = (packed >> (2 * which + 1)) & 1
    for copy in copies:
        copy.wait()


def own_kernel(info_ref, scenes_ref, *refs):
    *owns, sign_ref, sems = refs
    me = lax.axis_index("date")
    width = owns[0].shape[2]
    total = scenes_ref.shape[3]
    copies = []
    for which, own in enumerate(owns):
        is_upper = (me >> BITS[which]) & 1
        start = pl.multiple_of(is_upper * (total - width), 128)
        copy = pltpu.make_async_copy(
            scenes_ref.at[:, info_ref[2 * which], :, pl.ds(start, width)], own, sems.at[which]
        )
        copy.start()
        copies.append(copy)
        sign = jnp.where(info_ref[2 * which + 1] == 1, 1.0, -1.0).astype(F32)
        sign_ref[which] = jnp.full(sign_ref.shape[1:], sign, F32)
    for copy in copies:
        copy.wait()


def coef_kernel(pairs_ref, rows_ref, coef_ref):
    block = pairs_ref.shape[1] // 3
    groups = 2 * block
    for which in range(3):

        def step(slot, carry):
            pair = which * block + slot
            first = pairs_ref[0, pair] >> 1
            second = pairs_ref[1, pair] >> 1
            for date in range(2):
                value = rows_ref[date, pair]
                base = (which * 2 + date) * groups
                coef_ref[base + first] = value
                coef_ref[base + second] = value
            return carry

        lax.fori_loop(0, block, step, 0, unroll=8)


def coherence_kernel(matchings, sign_ref, *refs):
    count = len(matchings)
    recvs = refs[:count]
    owns = refs[count : 2 * count]
    out_ref, flat = refs[2 * count :]
    width = recvs[0].shape[2]
    lane = lax.broadcasted_iota(jnp.int32, (256, 128), 0)
    column = lax.broadcasted_iota(jnp.int32, (256, 128), 1)
    pool = jnp.where((lane & 127) >> 4 == column, 1.0, 0.0).astype(BF)
    flat[...] = jnp.zeros_like(flat)
    tiles = width // 128
    for slot, which in enumerate(matchings):
        acc0 = None
        acc1 = None
        for tile in range(tiles):
            cols = slice(tile * 128, tile * 128 + 128)
            a0 = owns[slot][0, :, cols].astype(F32)
            a1 = owns[slot][1, :, cols].astype(F32)
            b0 = recvs[slot][0, :, cols].astype(F32)
            b1 = recvs[slot][1, :, cols].astype(F32)
            terms = jnp.concatenate(
                [a0 * b0 + a1 * b1, a1 * b0 - a0 * b1, a0 * a0 + a1 * a1, b0 * b0 + b1 * b1],
                axis=0,
            )
            high = terms.astype(BF)
            low = (terms - high.astype(F32)).astype(BF)
            part = jnp.dot(
                jnp.concatenate([high, low], axis=1), pool, preferred_element_type=F32
            )
            if tile == 0:
                acc0 = part
            elif tile < 16:
                acc0 = acc0 + pltpu.roll(part, 8 * tile, 1)
            else:
                acc1 = part
        sign = sign_ref[which][None]
        for left, acc in ((0, acc0), (128, acc1)):
            grouped = acc.reshape(16, 8, 128)
            grouped = grouped + pltpu.roll(grouped, 7, 1)
            grouped = grouped + pltpu.roll(grouped, 6, 1)
            real, imag, power_a, power_b = (grouped[4 * i : 4 * i + 4] for i in range(4))
            scale = lax.rsqrt(power_a * power_b + 1e-06)
            real = real * scale
            imag = imag * (scale * sign)
            size = min(128, PITCH - left)
            for row in range(STRIP_ROWS):
                at = (row % 2) * (FLAT // 2) + (row // 2) * PITCH + left
                sub = 4 * (row % 2)
                for channel, value in ((0, real), (1, imag)):
                    line = 2 * slot + channel
                    flat[line : line + 1, at : at + size] = value[
                        row // 2, sub : sub + 1, :size
                    ]
    out_ref[...] = flat[...].astype(BF)


def conv_kernel(
    matchings, own_ref, up_ref, down_ref, w1_ref, w2_ref, w4_ref, *refs
):
    out_ref, xs, taps, hidden_a, hidden_b, zs, mask_ref, phases = refs[-8:]
    others = refs[:-8]
    me = lax.axis_index("date")
    strip = lax.axis_index("strip")
    strips = lax.axis_size("strip")
    guard = 128
    lane = lax.broadcasted_iota(jnp.int32, (8, 2 * PART), 1).astype(F32)
    odd = jnp.where(lane >= PART, 1.0, 0.0).astype(F32)
    lane = lane - PART * odd
    row = jnp.floor((lane + 0.5) * (1.0 / PITCH))
    column = lane - row * PITCH
    row = 2.0 * row + odd + (strip * STRIP_ROWS - HALO).astype(F32)
    limit = float(strips * STRIP_ROWS)
    mask_ref[...] = jnp.where(
        (row >= 0.0) & (row < limit) & (column < PIECE_COLS), 1.0, 0.0
    ).astype(F32)
    edge = HALO // 2 * PITCH
    for part in range(2):
        base = part * PART
        half = part * (FLAT // 2)
        xs[:, base : base + edge] = up_ref[:, half + edge : half + 2 * edge].astype(F32)
        xs[:, base + edge : base + 3 * edge] = own_ref[:, half : half + 2 * edge].astype(F32)
        xs[:, base + 3 * edge : base + PART] = down_ref[:, half : half + edge].astype(F32)
    even = xs[:, :PART] * mask_ref[:, :PART]
    odd = xs[:, PART:] * mask_ref[:, PART:]
    sources = (
        (pltpu.roll(odd, PITCH, 1), even),
        (even, odd),
        (odd, pltpu.roll(even, PART - PITCH, 1)),
    )
    for p in range(3):
        for part in range(2):
            base = part * PART
            for q in range(3):
                k = 8 * (3 * p + q)
                value = sources[p][part]
                if q != 1:
                    value = pltpu.roll(value, 1 if q == 0 else PART - 1, 1)
                taps[k : k + 8, base : base + PART] = value.astype(BF)
    hidden_a[...] = jnp.zeros_like(hidden_a)
    hidden_b[...] = jnp.zeros_like(hidden_b)

    def masked(value, part, lo, hi):
        lo, hi = part * PART + lo, part * PART + hi
        rows = value.shape[0]
        value = jnp.maximum(value, 0.0).reshape(rows // 8, 8, hi - lo)
        value = value * mask_ref[:, lo:hi][None]
        return value.reshape(rows, hi - lo).astype(BF)

    def terms(hidden, weight, part, lo, hi):
        stacked = jnp.concatenate(
            [hidden[part, :, guard + lo + q - 1 : guard + hi + q - 1] for q in range(3)],
            axis=0,
        )
        value = jnp.dot(weight, stacked, preferred_element_type=F32)
        rows = value.shape[0] // 3
        return [value[p * rows : p * rows + rows] for p in range(3)]

    def joined(hidden, weight, ranges, outs):
        (e_lo, e_hi), (o_lo, o_hi) = ranges
        from_even = terms(hidden, weight, 0, e_lo, e_hi)
        from_odd = terms(hidden, weight, 1, o_lo, o_hi)
        lo, hi = outs[0]
        to_even = (
            from_even[1][:, lo - e_lo : hi - e_lo]
            + from_odd[2][:, lo - o_lo : hi - o_lo]
            + pltpu.roll(from_odd[0], PITCH, 1)[:, lo - o_lo : hi - o_lo]
        )
        lo, hi = outs[1]
        to_odd = (
            from_odd[1][:, lo - o_lo : hi - o_lo]
            + from_even[0][:, lo - e_lo : hi - e_lo]
            + pltpu.roll(from_even[2], e_hi - e_lo - PITCH, 1)[:, lo - e_lo : hi - e_lo]
        )
        return to_even, to_odd

    for slot, which in enumerate(matchings):
        for part, (lo, hi) in enumerate(((128, 1152), (0, 1024))):
            base = part * PART
            value = jnp.dot(
                w1_ref[slot], taps[:, base + lo : base + hi], preferred_element_type=F32
            )
            hidden_a[part, :, guard + lo : guard + hi] = masked(value, part, lo, hi)
        outs = ((128, 1024), (128, 1024))
        both = joined(hidden_a, w2_ref[0], ((128, 1152), (0, 1024)), outs)
        for part, (lo, hi) in enumerate(outs):
            hidden_b[part, :, guard + lo : guard + hi] = masked(both[part], part, lo, hi)
        outs = ((256, 1024), (128, 896))
        both = joined(hidden_b, w2_ref[1], ((128, 1024), (128, 1024)), outs)
        is_upper = (me >> BITS[which]) & 1
        for part, (lo, hi) in enumerate(outs):
            value = masked(both[part], part, lo, hi)
            value = jnp.dot(w4_ref[...], value, preferred_element_type=F32)
            value = (
                pltpu.roll(value[0:8], 1, 1)
                + value[8:16]
                + pltpu.roll(value[16:24], hi - lo - 1, 1)
            )
            zs[part] = jnp.where(is_upper == 1, pltpu.roll(value, hi - lo - 8, 1), value)
        for r in range(STRIP_ROWS):
            at = (r // 2 + HALO // 2) * PITCH
            if r % 2 == 0:
                picks = ((0, 1, 0), (1, 2, 0), (1, 0, -PITCH))
            else:
                picks = ((1, 1, 0), (0, 0, 0), (0, 2, PITCH))
            total = None
            for part, p, move in picks:
                start = at + move - outs[part][0]
                value = zs[part, p : p + 1, start : start + 128]
                total = value if total is None else total + value
            phases[r : r + 1, :] = total
        phase = phases[...].astype(BF)
        if len(out_ref.shape) == 3:
            out_ref[slot] = phase
        else:
            for target in range(out_ref.shape[0]):
                out_ref[target, which] = phase
    if len(out_ref.shape) == 4:
        rest = [which for which in range(3) if which not in matchings]
        for which, phase_ref in zip(rest, others):
            phase = phase_ref[0]
            for target in range(out_ref.shape[0]):
                out_ref[target, which] = phase


def sum_kernel(coef_ref, gathered_ref, out_ref):
    groups = gathered_ref.shape[0]
    acc = [[jnp.zeros((8, 128), F32) for _ in range(2)] for _ in range(2)]
    for group in range(groups):
        for which in range(3):
            side = group >> BITS[which] & 1
            phase = gathered_ref[group, which].astype(F32)
            for date in range(2):
                coef = coef_ref[(which * 2 + date) * groups + group]
                acc[date][side] = acc[date][side] + coef * phase
    for date in range(2):
        for side in range(2):
            out_ref[date, :, side * 128 : side * 128 + 128] = acc[date][side]


def per_device(scenes, date_pairs, first_weight, mid_weight, last_weight, inversion):
    groups = lax.axis_size("date")
    strips = lax.axis_size("strip")
    me = lax.axis_index("date").astype(jnp.int32)
    width = PIECE_COLS * LOOK_C
    rows = scenes.shape[2]
    ch = first_weight.shape[2]
    pairs = date_pairs.T

    piece = (2, rows, width)
    *sends, info = pl.pallas_call(
        prep_kernel,
        name="prep",
        out_shape=[pltpu.VMEM(piece, BF)] * 3 + [jax.ShapeDtypeStruct((8,), jnp.int32)],
        in_specs=[spec(VMEM), spec(pl.ANY)],
        out_specs=[spec(VMEM)] * 3 + [spec(SMEM)],
        scratch_shapes=[pltpu.SemaphoreType.DMA((3,))],
    )(pairs, scenes)
    *owns, signs = pl.pallas_call(
        own_kernel,
        name="own",
        out_shape=[pltpu.VMEM(piece, BF)] * 3 + [pltpu.VMEM((3, 8, 128), F32)],
        in_specs=[spec(SMEM), spec(pl.ANY)],
        out_specs=[spec(VMEM)] * 4,
        scratch_shapes=[pltpu.SemaphoreType.DMA((3,))],
    )(info, scenes)

    recvs = {}
    for slot, which in enumerate(SWAPS):
        route = [(low, low ^ 1 << BITS[which]) for low in range(groups)]
        recvs[which] = lax.ppermute(sends[slot], "date", route)

    own_rows = lax.dynamic_slice_in_dim(inversion, 2 * me, 2, axis=0)
    coef = pl.pallas_call(
        coef_kernel,
        name="coef",
        out_shape=jax.ShapeDtypeStruct((6 * groups,), F32),
        in_specs=[spec(SMEM), spec(SMEM)],
        out_specs=spec(SMEM),
        cost_estimate=pl.CostEstimate(flops=2000000, bytes_accessed=4000000, transcendentals=0),
    )(pairs, own_rows)

    w1 = jnp.transpose(first_weight, (2, 0, 1, 3)).reshape(ch, 9, 2)
    w1 = jnp.stack(
        [jnp.pad(w1, ((0, 0), (0, 0), (2 * m, 6 - 2 * m))).reshape(ch, 72) for m in range(2)]
    )
    w2 = jnp.transpose(mid_weight, (0, 1, 3, 2, 4)).reshape(2, 3 * ch, 3 * ch)
    w4 = jnp.transpose(last_weight[:, :, 0], (1, 0, 2))
    w4 = jnp.pad(w4, ((0, 0), (0, 5), (0, 0))).reshape(24, ch)

    def looked_of(matchings):
        count = len(matchings)
        looked = pl.pallas_call(
            functools.partial(coherence_kernel, matchings),
            out_shape=pltpu.VMEM((8, FLAT), BF),
            in_specs=[spec(VMEM)] * (1 + 2 * count),
            out_specs=spec(VMEM),
            scratch_shapes=[pltpu.VMEM((8, FLAT), F32)],
        )(
            in_vmem(signs),
            *[in_vmem(recvs[which]) for which in matchings],
            *[in_vmem(owns[which]) for which in matchings],
        )
        up = lax.ppermute(looked, "strip", [(i, (i + 1) % strips) for i in range(strips)])
        down = lax.ppermute(looked, "strip", [((i + 1) % strips, i) for i in range(strips)])
        return looked, up, down

    def phases_of(matchings, looked, shape, *more):
        return pl.pallas_call(
            functools.partial(conv_kernel, matchings),
            out_shape=pltpu.VMEM(shape, BF),
            in_specs=[spec(VMEM)] * (6 + len(more)),
            out_specs=spec(VMEM),
            scratch_shapes=[
                pltpu.VMEM((8, EXT), F32),
                pltpu.VMEM((72, EXT), BF),
                pltpu.VMEM((2, ch, PART + 256), BF),
                pltpu.VMEM((2, ch, PART + 256), BF),
                pltpu.VMEM((2, 8, 768), F32),
                pltpu.VMEM((8, EXT), F32),
                pltpu.VMEM((8, 128), F32),
            ],
        )(
            *[in_vmem(v) for v in looked], *[in_vmem(v) for v in (w1, w2, w4)],
            *[in_vmem(v) for v in more],
        )

    done = []
    looked = [looked_of(group) for group in GROUPS]
    for group, value in zip(GROUPS, looked):
        if group is not GROUPS[-1]:
            shape = (len(group), STRIP_ROWS, 128)
            done.append(phases_of(group, value, shape))
    by_matching = {group[0]: value for group, value in zip(GROUPS, done)}
    rest = [by_matching[which] for which in sorted(by_matching)]
    shape = (groups, 3, STRIP_ROWS, 128)
    phases = phases_of(GROUPS[-1], looked[-1], shape, *rest)

    gathered = lax.all_to_all(phases, "date", 0, 0, tiled=True)

    return pl.pallas_call(
        sum_kernel,
        name="sums",
        out_shape=jax.ShapeDtypeStruct((2, STRIP_ROWS, 256), F32),
        in_specs=[spec(SMEM), spec(VMEM)],
        out_specs=spec(VMEM),
    )(coef, in_vmem(gathered))


def solution(mesh):
    return jax.shard_map(
        per_device,
        mesh=mesh,
        in_specs=(P(None, "date", "strip", None), P(), P(), P(), P(), P()),
        out_specs=P("date", "strip", None),
        check_vma=False,
    )
```

```python
import functools

import jax
import jax.numpy as jnp
from jax import lax
from jax.experimental import pallas as pl
from jax.experimental.pallas import tpu as pltpu
from jax.sharding import PartitionSpec as P


BF = jnp.bfloat16
F32 = jnp.float32
LOOK_C = 16
HALO = 4
PITCH = 144
PIECE_COLS = 136
STRIP_ROWS = 8
FLAT = STRIP_ROWS * PITCH
EXT = (STRIP_ROWS + 2 * HALO) * PITCH
BITS = (0, 1, 5)
SWAPS = (2, 1, 0)
GROUPS = ((2,), (0, 1))
PART = 8 * PITCH
SMEM = pltpu.SMEM
VMEM = pltpu.VMEM


def in_vmem(x):
    return pltpu.with_memory_space_constraint(x, pltpu.VMEM)


def spec(space):
    return pl.BlockSpec(memory_space=space)


def pieces(scenes_ref, date, start, target, sem):
    width = target.shape[2]
    copy = pltpu.make_async_copy(scenes_ref.at[:, date, :, pl.ds(start, width)], target, sem)
    copy.start()
    return [copy]


def prep_kernel(pairs_ref, scenes_ref, *refs):
    *sends, info_ref, sems = refs
    me = lax.axis_index("date")
    both = pairs_ref[...]
    block = both.shape[1] // 3
    lane = lax.broadcasted_iota(jnp.int32, both.shape, 1)
    side = lax.broadcasted_iota(jnp.int32, both.shape, 0)
    code = (both & 1) + jnp.where(side == 0, 2, 0)
    weight = jnp.where(lane < block, 1, jnp.where(lane < 2 * block, 4, 16))
    code = jnp.where((both >> 1) == me, code * weight, 0).astype(F32)
    packed = jnp.sum(code).astype(jnp.int32)
    width = sends[0].shape[2]
    total = scenes_ref.shape[3]
    copies = []
    for slot, which in enumerate(SWAPS):
        local = (packed >> (2 * which)) & 1
        is_upper = (me >> BITS[which]) & 1
        start = pl.multiple_of((1 - is_upper) * (total - width), 128)
        copies += pieces(scenes_ref, local, start, sends[slot], sems.at[slot])
        info_ref[2 * which] = local
        info_ref[2 * which + 1] = (packed >> (2 * which + 1)) & 1
    for copy in copies:
        copy.wait()


def own_kernel(info_ref, scenes_ref, *refs):
    *owns, sign_ref, sems = refs
    me = lax.axis_index("date")
    width = owns[0].shape[2]
    total = scenes_ref.shape[3]
    copies = []
    for which, own in enumerate(owns):
        is_upper = (me >> BITS[which]) & 1
        start = pl.multiple_of(is_upper * (total - width), 128)
        copies += pieces(scenes_ref, info_ref[2 * which], start, own, sems.at[which])
        sign = jnp.where(info_ref[2 * which + 1] == 1, 1.0, -1.0).astype(F32)
        sign_ref[which] = jnp.full(sign_ref.shape[1:], sign, F32)
    for copy in copies:
        copy.wait()


def coef_kernel(pairs_ref, inversion_ref, coef_ref):
    me = lax.axis_index("date")
    block = pairs_ref.shape[1] // 3
    groups = 2 * block
    dates = (2 * me, 2 * me + 1, 2 * (me ^ block), 2 * (me ^ block) + 1)
    for which in range(3):

        def step(slot, carry):
            pair = which * block + slot
            first = pairs_ref[0, pair] >> 1
            second = pairs_ref[1, pair] >> 1
            for place, date in enumerate(dates):
                value = inversion_ref[pair, date]
                base = (which * 4 + place) * groups
                coef_ref[base + first] = value
                coef_ref[base + second] = value
            return carry

        lax.fori_loop(0, block, step, 0, unroll=8)


def coherence_kernel(matchings, sign_ref, *refs):
    count = len(matchings)
    recvs = refs[:count]
    owns = refs[count : 2 * count]
    out_ref, flat = refs[2 * count :]
    width = recvs[0].shape[2]
    lane = lax.broadcasted_iota(jnp.int32, (256, 128), 0)
    column = lax.broadcasted_iota(jnp.int32, (256, 128), 1)
    pool = jnp.where((lane & 127) >> 4 == column, 1.0, 0.0).astype(BF)
    flat[...] = jnp.zeros_like(flat)
    tiles = width // 128
    for slot, which in enumerate(matchings):
        acc0 = None
        acc1 = None
        for tile in range(tiles):
            cols = slice(tile * 128, tile * 128 + 128)
            a0 = owns[slot][0, :, cols].astype(F32)
            a1 = owns[slot][1, :, cols].astype(F32)
            b0 = recvs[slot][0, :, cols].astype(F32)
            b1 = recvs[slot][1, :, cols].astype(F32)
            terms = jnp.concatenate(
                [a0 * b0 + a1 * b1, a1 * b0 - a0 * b1, a0 * a0 + a1 * a1, b0 * b0 + b1 * b1],
                axis=0,
            )
            high = terms.astype(BF)
            low = (terms - high.astype(F32)).astype(BF)
            part = jnp.dot(
                jnp.concatenate([high, low], axis=1), pool, preferred_element_type=F32
            )
            if tile == 0:
                acc0 = part
            elif tile < 16:
                acc0 = acc0 + pltpu.roll(part, 8 * tile, 1)
            else:
                acc1 = part
        sign = sign_ref[which][None]
        for left, acc in ((0, acc0), (128, acc1)):
            grouped = acc.reshape(16, 8, 128)
            grouped = grouped + pltpu.roll(grouped, 7, 1)
            grouped = grouped + pltpu.roll(grouped, 6, 1)
            real, imag, power_a, power_b = (grouped[4 * i : 4 * i + 4] for i in range(4))
            scale = lax.rsqrt(power_a * power_b + 1e-06)
            real = real * scale
            imag = imag * (scale * sign)
            size = min(128, PITCH - left)
            for row in range(STRIP_ROWS):
                at = (row % 2) * (FLAT // 2) + (row // 2) * PITCH + left
                sub = 4 * (row % 2)
                for channel, value in ((0, real), (1, imag)):
                    line = 2 * slot + channel
                    flat[line : line + 1, at : at + size] = value[
                        row // 2, sub : sub + 1, :size
                    ]
    out_ref[...] = flat[...].astype(BF)


def conv_kernel(
    matchings, own_ref, up_ref, down_ref, w1_ref, w2_ref, w4_ref, *refs
):
    out_ref, xs, taps, hidden_a, hidden_b, zs, mask_ref, phases = refs[-8:]
    others = refs[:-8]
    me = lax.axis_index("date")
    strip = lax.axis_index("strip")
    strips = lax.axis_size("strip")
    guard = 128
    lane = lax.broadcasted_iota(jnp.int32, (8, 2 * PART), 1).astype(F32)
    odd = jnp.where(lane >= PART, 1.0, 0.0).astype(F32)
    lane = lane - PART * odd
    row = jnp.floor((lane + 0.5) * (1.0 / PITCH))
    column = lane - row * PITCH
    row = 2.0 * row + odd + (strip * STRIP_ROWS - HALO).astype(F32)
    limit = float(strips * STRIP_ROWS)
    mask_ref[...] = jnp.where(
        (row >= 0.0) & (row < limit) & (column < PIECE_COLS), 1.0, 0.0
    ).astype(F32)
    edge = HALO // 2 * PITCH
    for part in range(2):
        base = part * PART
        half = part * (FLAT // 2)
        xs[:, base : base + edge] = up_ref[:, half + edge : half + 2 * edge].astype(F32)
        xs[:, base + edge : base + 3 * edge] = own_ref[:, half : half + 2 * edge].astype(F32)
        xs[:, base + 3 * edge : base + PART] = down_ref[:, half : half + edge].astype(F32)
    even = xs[:, :PART] * mask_ref[:, :PART]
    odd = xs[:, PART:] * mask_ref[:, PART:]
    sources = (
        (pltpu.roll(odd, PITCH, 1), even),
        (even, odd),
        (odd, pltpu.roll(even, PART - PITCH, 1)),
    )
    for p in range(3):
        for part in range(2):
            base = part * PART
            for q in range(3):
                k = 8 * (3 * p + q)
                value = sources[p][part]
                if q != 1:
                    value = pltpu.roll(value, 1 if q == 0 else PART - 1, 1)
                taps[k : k + 8, base : base + PART] = value.astype(BF)
    hidden_a[...] = jnp.zeros_like(hidden_a)
    hidden_b[...] = jnp.zeros_like(hidden_b)

    def masked(value, part, lo, hi):
        lo, hi = part * PART + lo, part * PART + hi
        rows = value.shape[0]
        value = jnp.maximum(value, 0.0).reshape(rows // 8, 8, hi - lo)
        value = value * mask_ref[:, lo:hi][None]
        return value.reshape(rows, hi - lo).astype(BF)

    def terms(hidden, weight, part, lo, hi):
        stacked = jnp.concatenate(
            [hidden[part, :, guard + lo + q - 1 : guard + hi + q - 1] for q in range(3)],
            axis=0,
        )
        value = jnp.dot(weight, stacked, preferred_element_type=F32)
        rows = value.shape[0] // 3
        return [value[p * rows : p * rows + rows] for p in range(3)]

    def joined(hidden, weight, ranges, outs):
        (e_lo, e_hi), (o_lo, o_hi) = ranges
        from_even = terms(hidden, weight, 0, e_lo, e_hi)
        from_odd = terms(hidden, weight, 1, o_lo, o_hi)
        lo, hi = outs[0]
        to_even = (
            from_even[1][:, lo - e_lo : hi - e_lo]
            + from_odd[2][:, lo - o_lo : hi - o_lo]
            + pltpu.roll(from_odd[0], PITCH, 1)[:, lo - o_lo : hi - o_lo]
        )
        lo, hi = outs[1]
        to_odd = (
            from_odd[1][:, lo - o_lo : hi - o_lo]
            + from_even[0][:, lo - e_lo : hi - e_lo]
            + pltpu.roll(from_even[2], e_hi - e_lo - PITCH, 1)[:, lo - e_lo : hi - e_lo]
        )
        return to_even, to_odd

    slots = range(len(matchings))
    for slot in slots:
        for part, (lo, hi) in enumerate(((128, 1152), (0, 1024))):
            base = part * PART
            value = jnp.dot(
                w1_ref[slot], taps[:, base + lo : base + hi], preferred_element_type=F32
            )
            hidden_a[slot, part, :, guard + lo : guard + hi] = masked(value, part, lo, hi)
    outs = ((128, 1024), (128, 1024))
    for slot in slots:
        both = joined(hidden_a.at[slot], w2_ref[0], ((128, 1152), (0, 1024)), outs)
        for part, (lo, hi) in enumerate(outs):
            hidden_b[slot, part, :, guard + lo : guard + hi] = masked(both[part], part, lo, hi)
    outs = ((256, 1024), (128, 896))
    for slot, which in enumerate(matchings):
        both = joined(hidden_b.at[slot], w2_ref[1], ((128, 1024), (128, 1024)), outs)
        is_upper = (me >> BITS[which]) & 1
        for part, (lo, hi) in enumerate(outs):
            value = masked(both[part], part, lo, hi)
            value = jnp.dot(w4_ref[...], value, preferred_element_type=F32)
            value = (
                pltpu.roll(value[0:8], 1, 1)
                + value[8:16]
                + pltpu.roll(value[16:24], hi - lo - 1, 1)
            )
            zs[slot, part] = jnp.where(is_upper == 1, pltpu.roll(value, hi - lo - 8, 1), value)
    for slot, which in enumerate(matchings):
        for r in range(STRIP_ROWS):
            at = (r // 2 + HALO // 2) * PITCH
            if r % 2 == 0:
                picks = ((0, 1, 0), (1, 2, 0), (1, 0, -PITCH))
            else:
                picks = ((1, 1, 0), (0, 0, 0), (0, 2, PITCH))
            total = None
            for part, p, move in picks:
                start = at + move - outs[part][0]
                value = zs[slot, part, p : p + 1, start : start + 128]
                total = value if total is None else total + value
            phases[slot, r : r + 1, :] = total
        phase = phases[slot].astype(BF)
        if len(out_ref.shape) == 3:
            out_ref[slot] = phase
        else:
            for target in range(out_ref.shape[0]):
                out_ref[target, which] = phase
    if len(out_ref.shape) == 4:
        rest = [which for which in range(3) if which not in matchings]
        for which, phase_ref in zip(rest, others):
            phase = phase_ref[0]
            for target in range(out_ref.shape[0]):
                out_ref[target, which] = phase


def sum_kernel(coef_ref, gathered_ref, mine_ref, other_ref):
    me = lax.axis_index("date")
    half = gathered_ref.shape[0]
    groups = 2 * half
    is_upper = me // half
    zero = jnp.zeros((8, 128), F32)
    sides = [[zero, zero] for _ in range(4)]
    own_side = [zero] * 4
    for source in range(half):
        for which in range(3):
            phase = gathered_ref[source, which].astype(F32)
            for place in range(4):
                coef = coef_ref[(which * 4 + place) * groups + is_upper * half + source]
                if which == 2:
                    own_side[place] = own_side[place] + coef * phase
                else:
                    side = source >> BITS[which] & 1
                    sides[place][side] = sides[place][side] + coef * phase
    for place in range(4):
        out = mine_ref if place < 2 else other_ref
        for side in range(2):
            value = sides[place][side] + jnp.where(is_upper == side, own_side[place], zero)
            out[place % 2, :, side * 128 : side * 128 + 128] = value


def per_device(scenes, date_pairs, first_weight, mid_weight, last_weight, inversion):
    groups = lax.axis_size("date")
    strips = lax.axis_size("strip")
    width = PIECE_COLS * LOOK_C
    rows = scenes.shape[2]
    ch = first_weight.shape[2]
    pairs = date_pairs.T

    piece = (2, rows, width)
    *sends, info = pl.pallas_call(
        prep_kernel,
        name="prep",
        out_shape=[pltpu.VMEM(piece, BF)] * 3 + [jax.ShapeDtypeStruct((8,), jnp.int32)],
        in_specs=[spec(VMEM), spec(pl.ANY)],
        out_specs=[spec(VMEM)] * 3 + [spec(SMEM)],
        scratch_shapes=[pltpu.SemaphoreType.DMA((3,))],
    )(pairs, scenes)
    *owns, signs = pl.pallas_call(
        own_kernel,
        name="own",
        out_shape=[pltpu.VMEM(piece, BF)] * 3 + [pltpu.VMEM((3, 8, 128), F32)],
        in_specs=[spec(SMEM), spec(pl.ANY)],
        out_specs=[spec(VMEM)] * 4,
        scratch_shapes=[pltpu.SemaphoreType.DMA((3,))],
    )(info, scenes)

    recvs = {}
    for slot, which in enumerate(SWAPS):
        route = [(low, low ^ 1 << BITS[which]) for low in range(groups)]
        recvs[which] = lax.ppermute(sends[slot], "date", route)

    coef = pl.pallas_call(
        coef_kernel,
        name="coef",
        out_shape=jax.ShapeDtypeStruct((12 * groups,), F32),
        in_specs=[spec(SMEM), spec(SMEM)],
        out_specs=spec(SMEM),
        cost_estimate=pl.CostEstimate(flops=2000000, bytes_accessed=4000000, transcendentals=0),
    )(pairs, inversion.T)

    w1 = jnp.transpose(first_weight, (2, 0, 1, 3)).reshape(ch, 9, 2)
    w1 = jnp.stack(
        [jnp.pad(w1, ((0, 0), (0, 0), (2 * m, 6 - 2 * m))).reshape(ch, 72) for m in range(2)]
    )
    w2 = jnp.transpose(mid_weight, (0, 1, 3, 2, 4)).reshape(2, 3 * ch, 3 * ch)
    w4 = jnp.transpose(last_weight[:, :, 0], (1, 0, 2))
    w4 = jnp.pad(w4, ((0, 0), (0, 5), (0, 0))).reshape(24, ch)

    def looked_of(matchings):
        count = len(matchings)
        looked = pl.pallas_call(
            functools.partial(coherence_kernel, matchings),
            out_shape=pltpu.VMEM((8, FLAT), BF),
            in_specs=[spec(VMEM)] * (1 + 2 * count),
            out_specs=spec(VMEM),
            scratch_shapes=[pltpu.VMEM((8, FLAT), F32)],
        )(
            in_vmem(signs),
            *[in_vmem(recvs[which]) for which in matchings],
            *[in_vmem(owns[which]) for which in matchings],
        )
        up = lax.ppermute(looked, "strip", [(i, (i + 1) % strips) for i in range(strips)])
        down = lax.ppermute(looked, "strip", [((i + 1) % strips, i) for i in range(strips)])
        return looked, up, down

    def phases_of(matchings, looked, shape, *more):
        return pl.pallas_call(
            functools.partial(conv_kernel, matchings),
            out_shape=pltpu.VMEM(shape, BF),
            in_specs=[spec(VMEM)] * (6 + len(more)),
            out_specs=spec(VMEM),
            scratch_shapes=[
                pltpu.VMEM((8, EXT), F32),
                pltpu.VMEM((72, EXT), BF),
                pltpu.VMEM((len(matchings), 2, ch, PART + 256), BF),
                pltpu.VMEM((len(matchings), 2, ch, PART + 256), BF),
                pltpu.VMEM((len(matchings), 2, 8, 768), F32),
                pltpu.VMEM((8, EXT), F32),
                pltpu.VMEM((len(matchings), 8, 128), F32),
            ],
        )(
            *[in_vmem(v) for v in looked], *[in_vmem(v) for v in (w1, w2, w4)],
            *[in_vmem(v) for v in more],
        )

    done = []
    looked = [looked_of(group) for group in GROUPS]
    for group, value in zip(GROUPS, looked):
        if group is not GROUPS[-1]:
            shape = (len(group), STRIP_ROWS, 128)
            done.append(phases_of(group, value, shape))
    by_matching = {group[0]: value for group, value in zip(GROUPS, done)}
    rest = [by_matching[which] for which in sorted(by_matching)]
    half = groups // 2
    shape = (half, 3, STRIP_ROWS, 128)
    phases = phases_of(GROUPS[-1], looked[-1], shape, *rest)

    halves = [list(range(half)), list(range(half, groups))]
    gathered = lax.all_to_all(phases, "date", 0, 0, tiled=True, axis_index_groups=halves)

    mine, other = pl.pallas_call(
        sum_kernel,
        name="sums",
        out_shape=[pltpu.VMEM((2, STRIP_ROWS, 256), F32)] * 2,
        in_specs=[spec(SMEM), spec(VMEM)],
        out_specs=[spec(VMEM)] * 2,
    )(coef, in_vmem(gathered))
    route = [(low, low ^ half) for low in range(groups)]
    return mine + lax.ppermute(other, "date", route)


def solution(mesh):
    return jax.shard_map(
        per_device,
        mesh=mesh,
        in_specs=(P(None, "date", "strip", None), P(), P(), P(), P(), P()),
        out_specs=P("date", "strip", None),
        check_vma=False,
    )
```

```python
import functools

import jax
import jax.numpy as jnp
from jax import lax
from jax.experimental import pallas as pl
from jax.experimental.pallas import tpu as pltpu
from jax.sharding import PartitionSpec as P


BF = jnp.bfloat16
F32 = jnp.float32
LOOK_C = 16
HALO = 4
PITCH = 144
PIECE_COLS = 136
STRIP_ROWS = 8
FLAT = STRIP_ROWS * PITCH
EXT = (STRIP_ROWS + 2 * HALO) * PITCH
BITS = (0, 1, 5)
SWAPS = (2, 1, 0)
GROUPS = ((2,), (0, 1))
PART = 8 * PITCH
SMEM = pltpu.SMEM
VMEM = pltpu.VMEM


def in_vmem(x):
    return pltpu.with_memory_space_constraint(x, pltpu.VMEM)


def spec(space):
    return pl.BlockSpec(memory_space=space)


def pieces(scenes_ref, date, start, target, sem):
    width = target.shape[2]
    copy = pltpu.make_async_copy(scenes_ref.at[:, date, :, pl.ds(start, width)], target, sem)
    copy.start()
    return [copy]


def packed_dates(pairs_ref, me):
    both = pairs_ref[...]
    block = both.shape[1] // 3
    lane = lax.broadcasted_iota(jnp.int32, both.shape, 1)
    side = lax.broadcasted_iota(jnp.int32, both.shape, 0)
    code = (both & 1) + jnp.where(side == 0, 2, 0)
    weight = jnp.where(lane < block, 1, jnp.where(lane < 2 * block, 4, 16))
    code = jnp.where((both >> 1) == me, code * weight, 0).astype(F32)
    return jnp.sum(code).astype(jnp.int32)


def prep_kernel(pairs_ref, scenes_ref, *refs):
    *sends, sems = refs
    me = lax.axis_index("date")
    packed = packed_dates(pairs_ref, me)
    width = sends[0].shape[2]
    total = scenes_ref.shape[3]
    copies = []
    for slot, which in enumerate(SWAPS):
        local = (packed >> (2 * which)) & 1
        is_upper = (me >> BITS[which]) & 1
        start = pl.multiple_of((1 - is_upper) * (total - width), 128)
        copies += pieces(scenes_ref, local, start, sends[slot], sems.at[slot])
    for copy in copies:
        copy.wait()


def own_kernel(pairs_ref, scenes_ref, *refs):
    *owns, sign_ref, sems = refs
    me = lax.axis_index("date")
    packed = packed_dates(pairs_ref, me)
    width = owns[0].shape[2]
    total = scenes_ref.shape[3]
    copies = []
    for which, own in enumerate(owns):
        is_upper = (me >> BITS[which]) & 1
        start = pl.multiple_of(is_upper * (total - width), 128)
        local = (packed >> (2 * which)) & 1
        copies += pieces(scenes_ref, local, start, own, sems.at[which])
        is_ref = (packed >> (2 * which + 1)) & 1
        sign = jnp.where(is_ref == 1, 1.0, -1.0).astype(F32)
        sign_ref[which] = jnp.full(sign_ref.shape[1:], sign, F32)
    for copy in copies:
        copy.wait()


def coef_kernel(pairs_ref, inversion_ref, coef_ref):
    me = lax.axis_index("date")
    block = pairs_ref.shape[1] // 3
    groups = 2 * block
    dates = (2 * me, 2 * me + 1, 2 * (me ^ block), 2 * (me ^ block) + 1)
    for which in range(3):

        def step(slot, carry):
            pair = which * block + slot
            first = pairs_ref[0, pair] >> 1
            second = pairs_ref[1, pair] >> 1
            for place, date in enumerate(dates):
                value = inversion_ref[pair, date]
                base = (which * 4 + place) * groups
                coef_ref[base + first] = value
                coef_ref[base + second] = value
            return carry

        lax.fori_loop(0, block, step, 0, unroll=8)


def coherence_kernel(matchings, sign_ref, *refs):
    count = len(matchings)
    recvs = refs[:count]
    owns = refs[count : 2 * count]
    out_ref, flat = refs[2 * count :]
    width = recvs[0].shape[2]
    lane = lax.broadcasted_iota(jnp.int32, (256, 128), 0)
    column = lax.broadcasted_iota(jnp.int32, (256, 128), 1)
    pool = jnp.where((lane & 127) >> 4 == column, 1.0, 0.0).astype(BF)
    flat[...] = jnp.zeros_like(flat)
    tiles = width // 128
    for slot, which in enumerate(matchings):
        acc0 = None
        acc1 = None
        for tile in range(tiles):
            cols = slice(tile * 128, tile * 128 + 128)
            a0 = owns[slot][0, :, cols].astype(F32)
            a1 = owns[slot][1, :, cols].astype(F32)
            b0 = recvs[slot][0, :, cols].astype(F32)
            b1 = recvs[slot][1, :, cols].astype(F32)
            terms = jnp.concatenate(
                [a0 * b0 + a1 * b1, a1 * b0 - a0 * b1, a0 * a0 + a1 * a1, b0 * b0 + b1 * b1],
                axis=0,
            )
            high = terms.astype(BF)
            low = (terms - high.astype(F32)).astype(BF)
            part = jnp.dot(
                jnp.concatenate([high, low], axis=1), pool, preferred_element_type=F32
            )
            if tile == 0:
                acc0 = part
            elif tile < 16:
                acc0 = acc0 + pltpu.roll(part, 8 * tile, 1)
            else:
                acc1 = part
        sign = sign_ref[which][None]
        for left, acc in ((0, acc0), (128, acc1)):
            grouped = acc.reshape(16, 8, 128)
            grouped = grouped + pltpu.roll(grouped, 7, 1)
            grouped = grouped + pltpu.roll(grouped, 6, 1)
            real, imag, power_a, power_b = (grouped[4 * i : 4 * i + 4] for i in range(4))
            scale = lax.rsqrt(power_a * power_b + 1e-06)
            real = real * scale
            imag = imag * (scale * sign)
            size = min(128, PITCH - left)
            for row in range(STRIP_ROWS):
                at = (row % 2) * (FLAT // 2) + (row // 2) * PITCH + left
                sub = 4 * (row % 2)
                for channel, value in ((0, real), (1, imag)):
                    line = 2 * slot + channel
                    flat[line : line + 1, at : at + size] = value[
                        row // 2, sub : sub + 1, :size
                    ]
    out_ref[...] = flat[...].astype(BF)


def conv_kernel(
    matchings, own_ref, up_ref, down_ref, w1_ref, w2_ref, w4_ref, *refs
):
    out_ref, xs, taps, hidden_a, hidden_b, zs, mask_ref, phases = refs[-8:]
    others = refs[:-8]
    me = lax.axis_index("date")
    strip = lax.axis_index("strip")
    strips = lax.axis_size("strip")
    guard = 128
    lane = lax.broadcasted_iota(jnp.int32, (8, 2 * PART), 1).astype(F32)
    odd = jnp.where(lane >= PART, 1.0, 0.0).astype(F32)
    lane = lane - PART * odd
    row = jnp.floor((lane + 0.5) * (1.0 / PITCH))
    column = lane - row * PITCH
    row = 2.0 * row + odd + (strip * STRIP_ROWS - HALO).astype(F32)
    limit = float(strips * STRIP_ROWS)
    mask_ref[...] = jnp.where(
        (row >= 0.0) & (row < limit) & (column < PIECE_COLS), 1.0, 0.0
    ).astype(F32)
    edge = HALO // 2 * PITCH
    for part in range(2):
        base = part * PART
        half = part * (FLAT // 2)
        xs[:, base : base + edge] = up_ref[:, half + edge : half + 2 * edge].astype(F32)
        xs[:, base + edge : base + 3 * edge] = own_ref[:, half : half + 2 * edge].astype(F32)
        xs[:, base + 3 * edge : base + PART] = down_ref[:, half : half + edge].astype(F32)
    even = xs[:, :PART] * mask_ref[:, :PART]
    odd = xs[:, PART:] * mask_ref[:, PART:]
    sources = (
        (pltpu.roll(odd, PITCH, 1), even),
        (even, odd),
        (odd, pltpu.roll(even, PART - PITCH, 1)),
    )
    for p in range(3):
        for part in range(2):
            base = part * PART
            for q in range(3):
                k = 8 * (3 * p + q)
                value = sources[p][part]
                if q != 1:
                    value = pltpu.roll(value, 1 if q == 0 else PART - 1, 1)
                taps[k : k + 8, base : base + PART] = value.astype(BF)
    hidden_a[...] = jnp.zeros_like(hidden_a)
    hidden_b[...] = jnp.zeros_like(hidden_b)

    def masked(value, part, lo, hi):
        lo, hi = part * PART + lo, part * PART + hi
        rows = value.shape[0]
        value = jnp.maximum(value, 0.0).reshape(rows // 8, 8, hi - lo)
        value = value * mask_ref[:, lo:hi][None]
        return value.reshape(rows, hi - lo).astype(BF)

    def terms(hidden, weight, part, lo, hi):
        stacked = jnp.concatenate(
            [hidden[part, :, guard + lo + q - 1 : guard + hi + q - 1] for q in range(3)],
            axis=0,
        )
        value = jnp.dot(weight, stacked, preferred_element_type=F32)
        rows = value.shape[0] // 3
        return [value[p * rows : p * rows + rows] for p in range(3)]

    def joined(hidden, weight, ranges, outs):
        (e_lo, e_hi), (o_lo, o_hi) = ranges
        from_even = terms(hidden, weight, 0, e_lo, e_hi)
        from_odd = terms(hidden, weight, 1, o_lo, o_hi)
        lo, hi = outs[0]
        to_even = (
            from_even[1][:, lo - e_lo : hi - e_lo]
            + from_odd[2][:, lo - o_lo : hi - o_lo]
            + pltpu.roll(from_odd[0], PITCH, 1)[:, lo - o_lo : hi - o_lo]
        )
        lo, hi = outs[1]
        to_odd = (
            from_odd[1][:, lo - o_lo : hi - o_lo]
            + from_even[0][:, lo - e_lo : hi - e_lo]
            + pltpu.roll(from_even[2], e_hi - e_lo - PITCH, 1)[:, lo - e_lo : hi - e_lo]
        )
        return to_even, to_odd

    slots = range(len(matchings))
    for slot in slots:
        for part, (lo, hi) in enumerate(((128, 1152), (0, 1024))):
            base = part * PART
            value = jnp.dot(
                w1_ref[slot], taps[:, base + lo : base + hi], preferred_element_type=F32
            )
            hidden_a[slot, part, :, guard + lo : guard + hi] = masked(value, part, lo, hi)
    outs = ((128, 1024), (128, 1024))
    for slot in slots:
        both = joined(hidden_a.at[slot], w2_ref[0], ((128, 1152), (0, 1024)), outs)
        for part, (lo, hi) in enumerate(outs):
            hidden_b[slot, part, :, guard + lo : guard + hi] = masked(both[part], part, lo, hi)
    outs = ((256, 1024), (128, 896))
    for slot, which in enumerate(matchings):
        both = joined(hidden_b.at[slot], w2_ref[1], ((128, 1024), (128, 1024)), outs)
        is_upper = (me >> BITS[which]) & 1
        for part, (lo, hi) in enumerate(outs):
            value = masked(both[part], part, lo, hi)
            value = jnp.dot(w4_ref[...], value, preferred_element_type=F32)
            value = (
                pltpu.roll(value[0:8], 1, 1)
                + value[8:16]
                + pltpu.roll(value[16:24], hi - lo - 1, 1)
            )
            zs[slot, part] = jnp.where(is_upper == 1, pltpu.roll(value, hi - lo - 8, 1), value)
    for slot, which in enumerate(matchings):
        for r in range(STRIP_ROWS):
            at = (r // 2 + HALO // 2) * PITCH
            if r % 2 == 0:
                picks = ((0, 1, 0), (1, 2, 0), (1, 0, -PITCH))
            else:
                picks = ((1, 1, 0), (0, 0, 0), (0, 2, PITCH))
            total = None
            for part, p, move in picks:
                start = at + move - outs[part][0]
                value = zs[slot, part, p : p + 1, start : start + 128]
                total = value if total is None else total + value
            phases[slot, r : r + 1, :] = total
        phase = phases[slot].astype(BF)
        if len(out_ref.shape) == 3:
            out_ref[slot] = phase
        else:
            for target in range(out_ref.shape[0]):
                out_ref[target, which] = phase
    if len(out_ref.shape) == 4:
        rest = [which for which in range(3) if which not in matchings]
        for which, phase_ref in zip(rest, others):
            phase = phase_ref[0]
            for target in range(out_ref.shape[0]):
                out_ref[target, which] = phase


def sum_kernel(coef_ref, gathered_ref, mine_ref, other_ref):
    me = lax.axis_index("date")
    half = gathered_ref.shape[0]
    groups = 2 * half
    is_upper = me // half
    zero = jnp.zeros((8, 128), F32)
    sides = [[zero, zero] for _ in range(4)]
    own_side = [zero] * 4
    for source in range(half):
        for which in range(3):
            phase = gathered_ref[source, which].astype(F32)
            for place in range(4):
                coef = coef_ref[(which * 4 + place) * groups + is_upper * half + source]
                if which == 2:
                    own_side[place] = own_side[place] + coef * phase
                else:
                    side = source >> BITS[which] & 1
                    sides[place][side] = sides[place][side] + coef * phase
    for place in range(4):
        out = mine_ref if place < 2 else other_ref
        for side in range(2):
            value = sides[place][side] + jnp.where(is_upper == side, own_side[place], zero)
            out[place % 2, :, side * 128 : side * 128 + 128] = value


def per_device(scenes, date_pairs, first_weight, mid_weight, last_weight, inversion):
    groups = lax.axis_size("date")
    strips = lax.axis_size("strip")
    width = PIECE_COLS * LOOK_C
    rows = scenes.shape[2]
    ch = first_weight.shape[2]
    pairs = date_pairs.T

    piece = (2, rows, width)
    sends = pl.pallas_call(
        prep_kernel,
        name="prep",
        out_shape=[pltpu.VMEM(piece, BF)] * 3,
        in_specs=[spec(VMEM), spec(pl.ANY)],
        out_specs=[spec(VMEM)] * 3,
        scratch_shapes=[pltpu.SemaphoreType.DMA((3,))],
    )(pairs, scenes)
    *owns, signs = pl.pallas_call(
        own_kernel,
        name="own",
        out_shape=[pltpu.VMEM(piece, BF)] * 3 + [pltpu.VMEM((3, 8, 128), F32)],
        in_specs=[spec(VMEM), spec(pl.ANY)],
        out_specs=[spec(VMEM)] * 4,
        scratch_shapes=[pltpu.SemaphoreType.DMA((3,))],
    )(pairs, scenes)

    recvs = {}
    for slot, which in enumerate(SWAPS):
        route = [(low, low ^ 1 << BITS[which]) for low in range(groups)]
        recvs[which] = lax.ppermute(sends[slot], "date", route)

    coef = pl.pallas_call(
        coef_kernel,
        name="coef",
        out_shape=pltpu.SMEM((12 * groups,), F32),
        in_specs=[spec(SMEM), spec(SMEM)],
        out_specs=spec(SMEM),
        cost_estimate=pl.CostEstimate(flops=2000000, bytes_accessed=4000000, transcendentals=0),
    )(pairs, inversion.T)

    w1 = jnp.transpose(first_weight, (2, 0, 1, 3)).reshape(ch, 9, 2)
    w1 = jnp.stack(
        [jnp.pad(w1, ((0, 0), (0, 0), (2 * m, 6 - 2 * m))).reshape(ch, 72) for m in range(2)]
    )
    w2 = jnp.transpose(mid_weight, (0, 1, 3, 2, 4)).reshape(2, 3 * ch, 3 * ch)
    w4 = jnp.transpose(last_weight[:, :, 0], (1, 0, 2))
    w4 = jnp.pad(w4, ((0, 0), (0, 5), (0, 0))).reshape(24, ch)

    def looked_of(matchings):
        count = len(matchings)
        looked = pl.pallas_call(
            functools.partial(coherence_kernel, matchings),
            out_shape=pltpu.VMEM((8, FLAT), BF),
            in_specs=[spec(VMEM)] * (1 + 2 * count),
            out_specs=spec(VMEM),
            scratch_shapes=[pltpu.VMEM((8, FLAT), F32)],
        )(
            in_vmem(signs),
            *[in_vmem(recvs[which]) for which in matchings],
            *[in_vmem(owns[which]) for which in matchings],
        )
        up = lax.ppermute(looked, "strip", [(i, (i + 1) % strips) for i in range(strips)])
        down = lax.ppermute(looked, "strip", [((i + 1) % strips, i) for i in range(strips)])
        return looked, up, down

    def phases_of(matchings, looked, shape, *more):
        return pl.pallas_call(
            functools.partial(conv_kernel, matchings),
            out_shape=pltpu.VMEM(shape, BF),
            in_specs=[spec(VMEM)] * (6 + len(more)),
            out_specs=spec(VMEM),
            scratch_shapes=[
                pltpu.VMEM((8, EXT), F32),
                pltpu.VMEM((72, EXT), BF),
                pltpu.VMEM((len(matchings), 2, ch, PART + 256), BF),
                pltpu.VMEM((len(matchings), 2, ch, PART + 256), BF),
                pltpu.VMEM((len(matchings), 2, 8, 768), F32),
                pltpu.VMEM((8, EXT), F32),
                pltpu.VMEM((len(matchings), 8, 128), F32),
            ],
        )(
            *[in_vmem(v) for v in looked], *[in_vmem(v) for v in (w1, w2, w4)],
            *[in_vmem(v) for v in more],
        )

    done = []
    looked = [looked_of(group) for group in GROUPS]
    for group, value in zip(GROUPS, looked):
        if group is not GROUPS[-1]:
            shape = (len(group), STRIP_ROWS, 128)
            done.append(phases_of(group, value, shape))
    by_matching = {group[0]: value for group, value in zip(GROUPS, done)}
    rest = [by_matching[which] for which in sorted(by_matching)]
    half = groups // 2
    shape = (half, 3, STRIP_ROWS, 128)
    phases = phases_of(GROUPS[-1], looked[-1], shape, *rest)

    halves = [list(range(half)), list(range(half, groups))]
    gathered = lax.all_to_all(phases, "date", 0, 0, tiled=True, axis_index_groups=halves)

    mine, other = pl.pallas_call(
        sum_kernel,
        name="sums",
        out_shape=[pltpu.VMEM((2, STRIP_ROWS, 256), F32)] * 2,
        in_specs=[spec(SMEM), spec(VMEM)],
        out_specs=[spec(VMEM)] * 2,
    )(pltpu.with_memory_space_constraint(coef, pltpu.SMEM), in_vmem(gathered))
    route = [(low, low ^ half) for low in range(groups)]
    return mine + lax.ppermute(other, "date", route)


def solution(mesh):
    return jax.shard_map(
        per_device,
        mesh=mesh,
        in_specs=(P(None, "date", "strip", None), P(), P(), P(), P(), P()),
        out_specs=P("date", "strip", None),
        check_vma=False,
    )
```

```python
import functools

import jax
import jax.numpy as jnp
from jax import lax
from jax.experimental import pallas as pl
from jax.experimental.pallas import tpu as pltpu
from jax.sharding import PartitionSpec as P


BF = jnp.bfloat16
F32 = jnp.float32
LOOK_C = 16
HALO = 4
PITCH = 144
PIECE_COLS = 136
STRIP_ROWS = 8
FLAT = STRIP_ROWS * PITCH
EXT = (STRIP_ROWS + 2 * HALO) * PITCH
BITS = (0, 1, 5)
SWAPS = (2, 1, 0)
GROUPS = ((2,), (0, 1))
PART = 8 * PITCH
SMEM = pltpu.SMEM
VMEM = pltpu.VMEM


def in_vmem(x):
    return pltpu.with_memory_space_constraint(x, pltpu.VMEM)


def spec(space):
    return pl.BlockSpec(memory_space=space)


def pieces(scenes_ref, date, start, target, sem):
    width = target.shape[2]
    copy = pltpu.make_async_copy(scenes_ref.at[:, date, :, pl.ds(start, width)], target, sem)
    copy.start()
    return [copy]


def packed_dates(pairs_ref, me):
    both = pairs_ref[...]
    block = both.shape[1] // 3
    lane = lax.broadcasted_iota(jnp.int32, both.shape, 1)
    side = lax.broadcasted_iota(jnp.int32, both.shape, 0)
    code = (both & 1) + jnp.where(side == 0, 2, 0)
    weight = jnp.where(lane < block, 1, jnp.where(lane < 2 * block, 4, 16))
    code = jnp.where((both >> 1) == me, code * weight, 0).astype(F32)
    return jnp.sum(code).astype(jnp.int32)


def prep_kernel(pairs_ref, scenes_ref, *refs):
    *sends, sems = refs
    me = lax.axis_index("date")
    packed = packed_dates(pairs_ref, me)
    width = sends[0].shape[2]
    total = scenes_ref.shape[3]
    copies = []
    for slot, which in enumerate(SWAPS):
        local = (packed >> (2 * which)) & 1
        is_upper = (me >> BITS[which]) & 1
        start = pl.multiple_of((1 - is_upper) * (total - width), 128)
        copies += pieces(scenes_ref, local, start, sends[slot], sems.at[slot])
    for copy in copies:
        copy.wait()


def own_kernel(pairs_ref, scenes_ref, *refs):
    *owns, sign_ref, sems = refs
    me = lax.axis_index("date")
    packed = packed_dates(pairs_ref, me)
    width = owns[0].shape[2]
    total = scenes_ref.shape[3]
    copies = []
    for which, own in enumerate(owns):
        is_upper = (me >> BITS[which]) & 1
        start = pl.multiple_of(is_upper * (total - width), 128)
        local = (packed >> (2 * which)) & 1
        copies += pieces(scenes_ref, local, start, own, sems.at[which])
        is_ref = (packed >> (2 * which + 1)) & 1
        sign = jnp.where(is_ref == 1, 1.0, -1.0).astype(F32)
        sign_ref[which] = jnp.full(sign_ref.shape[1:], sign, F32)
    for copy in copies:
        copy.wait()


def coef_kernel(pairs_ref, inversion_ref, coef_ref):
    me = lax.axis_index("date")
    block = pairs_ref.shape[1] // 3
    groups = 2 * block
    dates = (2 * me, 2 * me + 1, 2 * (me ^ block), 2 * (me ^ block) + 1)
    for which in range(3):

        def step(slot, carry):
            pair = which * block + slot
            first = pairs_ref[0, pair] >> 1
            second = pairs_ref[1, pair] >> 1
            for place, date in enumerate(dates):
                value = inversion_ref[pair, date]
                base = (which * 4 + place) * groups
                coef_ref[base + first] = value
                coef_ref[base + second] = value
            return carry

        lax.fori_loop(0, block, step, 0, unroll=8)


def coherence_kernel(matchings, sign_ref, *refs):
    count = len(matchings)
    recvs = refs[:count]
    owns = refs[count : 2 * count]
    out_ref, flat = refs[2 * count :]
    width = recvs[0].shape[2]
    lane = lax.broadcasted_iota(jnp.int32, (256, 128), 0)
    column = lax.broadcasted_iota(jnp.int32, (256, 128), 1)
    pool = jnp.where((lane & 127) >> 4 == column, 1.0, 0.0).astype(BF)
    flat[...] = jnp.zeros_like(flat)
    tiles = width // 128
    for slot, which in enumerate(matchings):
        acc0 = None
        acc1 = None
        for tile in range(tiles):
            cols = slice(tile * 128, tile * 128 + 128)
            a0 = owns[slot][0, :, cols].astype(F32)
            a1 = owns[slot][1, :, cols].astype(F32)
            b0 = recvs[slot][0, :, cols].astype(F32)
            b1 = recvs[slot][1, :, cols].astype(F32)
            terms = jnp.concatenate(
                [a0 * b0 + a1 * b1, a1 * b0 - a0 * b1, a0 * a0 + a1 * a1, b0 * b0 + b1 * b1],
                axis=0,
            )
            high = terms.astype(BF)
            low = (terms - high.astype(F32)).astype(BF)
            part = jnp.dot(
                jnp.concatenate([high, low], axis=1), pool, preferred_element_type=F32
            )
            if tile == 0:
                acc0 = part
            elif tile < 16:
                acc0 = acc0 + pltpu.roll(part, 8 * tile, 1)
            else:
                acc1 = part
        sign = sign_ref[which][None]
        for left, acc in ((0, acc0), (128, acc1)):
            grouped = acc.reshape(16, 8, 128)
            grouped = grouped + pltpu.roll(grouped, 7, 1)
            grouped = grouped + pltpu.roll(grouped, 6, 1)
            real, imag, power_a, power_b = (grouped[4 * i : 4 * i + 4] for i in range(4))
            scale = lax.rsqrt(power_a * power_b + 1e-06)
            real = real * scale
            imag = imag * (scale * sign)
            size = min(128, PITCH - left)
            for row in range(STRIP_ROWS):
                at = (row % 2) * (FLAT // 2) + (row // 2) * PITCH + left
                sub = 4 * (row % 2)
                for channel, value in ((0, real), (1, imag)):
                    line = 2 * slot + channel
                    flat[line : line + 1, at : at + size] = value[
                        row // 2, sub : sub + 1, :size
                    ]
    out_ref[...] = flat[...].astype(BF)


def conv_kernel(
    matchings, own_ref, up_ref, down_ref, w1_ref, w2_ref, w4_ref, *refs
):
    out_ref, xs, taps, hidden_a, hidden_b, zs, mask_ref, phases = refs[-8:]
    others = refs[:-8]
    me = lax.axis_index("date")
    strip = lax.axis_index("strip")
    strips = lax.axis_size("strip")
    guard = 128
    lane = lax.broadcasted_iota(jnp.int32, (8, 2 * PART), 1).astype(F32)
    odd = jnp.where(lane >= PART, 1.0, 0.0).astype(F32)
    lane = lane - PART * odd
    row = jnp.floor((lane + 0.5) * (1.0 / PITCH))
    column = lane - row * PITCH
    row = 2.0 * row + odd + (strip * STRIP_ROWS - HALO).astype(F32)
    limit = float(strips * STRIP_ROWS)
    mask_ref[...] = jnp.where(
        (row >= 0.0) & (row < limit) & (column < PIECE_COLS), 1.0, 0.0
    ).astype(F32)
    edge = HALO // 2 * PITCH
    for part in range(2):
        base = part * PART
        half = part * (FLAT // 2)
        xs[:, base : base + edge] = up_ref[:, half + edge : half + 2 * edge].astype(F32)
        xs[:, base + edge : base + 3 * edge] = own_ref[:, half : half + 2 * edge].astype(F32)
        xs[:, base + 3 * edge : base + PART] = down_ref[:, half : half + edge].astype(F32)
    even = xs[:, :PART] * mask_ref[:, :PART]
    odd = xs[:, PART:] * mask_ref[:, PART:]
    sources = (
        (pltpu.roll(odd, PITCH, 1), even),
        (even, odd),
        (odd, pltpu.roll(even, PART - PITCH, 1)),
    )
    for p in range(3):
        for part in range(2):
            base = part * PART
            for q in range(3):
                k = 8 * (3 * p + q)
                value = sources[p][part]
                if q != 1:
                    value = pltpu.roll(value, 1 if q == 0 else PART - 1, 1)
                taps[k : k + 8, base : base + PART] = value.astype(BF)
    for hidden, written in (
        (hidden_a, ((128, 1152), (0, 1024))),
        (hidden_b, ((128, 1024), (128, 1024))),
    ):
        for part, (lo, hi) in enumerate(written):
            for start in (guard + lo - 128, guard + hi):
                side = hidden.shape[0], hidden.shape[2], 128
                hidden[:, part, :, start : start + 128] = jnp.zeros(side, BF)

    def masked(value, part, lo, hi):
        lo, hi = part * PART + lo, part * PART + hi
        rows = value.shape[0]
        value = jnp.maximum(value, 0.0).reshape(rows // 8, 8, hi - lo)
        value = value * mask_ref[:, lo:hi][None]
        return value.reshape(rows, hi - lo).astype(BF)

    def terms(hidden, weight, part, lo, hi):
        stacked = jnp.concatenate(
            [hidden[part, :, guard + lo + q - 1 : guard + hi + q - 1] for q in range(3)],
            axis=0,
        )
        value = jnp.dot(weight, stacked, preferred_element_type=F32)
        rows = value.shape[0] // 3
        return [value[p * rows : p * rows + rows] for p in range(3)]

    def joined(hidden, weight, ranges, outs):
        (e_lo, e_hi), (o_lo, o_hi) = ranges
        from_even = terms(hidden, weight, 0, e_lo, e_hi)
        from_odd = terms(hidden, weight, 1, o_lo, o_hi)
        lo, hi = outs[0]
        to_even = (
            from_even[1][:, lo - e_lo : hi - e_lo]
            + from_odd[2][:, lo - o_lo : hi - o_lo]
            + pltpu.roll(from_odd[0], PITCH, 1)[:, lo - o_lo : hi - o_lo]
        )
        lo, hi = outs[1]
        to_odd = (
            from_odd[1][:, lo - o_lo : hi - o_lo]
            + from_even[0][:, lo - e_lo : hi - e_lo]
            + pltpu.roll(from_even[2], e_hi - e_lo - PITCH, 1)[:, lo - e_lo : hi - e_lo]
        )
        return to_even, to_odd

    slots = range(len(matchings))
    for slot in slots:
        for part, (lo, hi) in enumerate(((128, 1152), (0, 1024))):
            base = part * PART
            value = jnp.dot(
                w1_ref[slot], taps[:, base + lo : base + hi], preferred_element_type=F32
            )
            hidden_a[slot, part, :, guard + lo : guard + hi] = masked(value, part, lo, hi)
    outs = ((128, 1024), (128, 1024))
    for slot in slots:
        both = joined(hidden_a.at[slot], w2_ref[0], ((128, 1152), (0, 1024)), outs)
        for part, (lo, hi) in enumerate(outs):
            hidden_b[slot, part, :, guard + lo : guard + hi] = masked(both[part], part, lo, hi)
    outs = ((256, 1024), (128, 896))
    for slot, which in enumerate(matchings):
        both = joined(hidden_b.at[slot], w2_ref[1], ((128, 1024), (128, 1024)), outs)
        is_upper = (me >> BITS[which]) & 1
        for part, (lo, hi) in enumerate(outs):
            value = masked(both[part], part, lo, hi)
            value = jnp.dot(w4_ref[...], value, preferred_element_type=F32)
            value = (
                pltpu.roll(value[0:8], 1, 1)
                + value[8:16]
                + pltpu.roll(value[16:24], hi - lo - 1, 1)
            )
            zs[slot, part] = jnp.where(is_upper == 1, pltpu.roll(value, hi - lo - 8, 1), value)
    for slot, which in enumerate(matchings):
        for r in range(STRIP_ROWS):
            at = (r // 2 + HALO // 2) * PITCH
            if r % 2 == 0:
                picks = ((0, 1, 0), (1, 2, 0), (1, 0, -PITCH))
            else:
                picks = ((1, 1, 0), (0, 0, 0), (0, 2, PITCH))
            total = None
            for part, p, move in picks:
                start = at + move - outs[part][0]
                value = zs[slot, part, p : p + 1, start : start + 128]
                total = value if total is None else total + value
            phases[slot, r : r + 1, :] = total
        phase = phases[slot].astype(BF)
        if len(out_ref.shape) == 3:
            out_ref[slot] = phase
        else:
            for target in range(out_ref.shape[0]):
                out_ref[target, which] = phase
    if len(out_ref.shape) == 4:
        rest = [which for which in range(3) if which not in matchings]
        for which, phase_ref in zip(rest, others):
            phase = phase_ref[0]
            for target in range(out_ref.shape[0]):
                out_ref[target, which] = phase


def sum_kernel(coef_ref, gathered_ref, mine_ref, other_ref):
    me = lax.axis_index("date")
    half = gathered_ref.shape[0]
    groups = 2 * half
    is_upper = me // half
    zero = jnp.zeros((8, 128), F32)
    sides = [[zero, zero] for _ in range(4)]
    own_side = [zero] * 4
    for source in range(half):
        for which in range(3):
            phase = gathered_ref[source, which].astype(F32)
            for place in range(4):
                coef = coef_ref[(which * 4 + place) * groups + is_upper * half + source]
                if which == 2:
                    own_side[place] = own_side[place] + coef * phase
                else:
                    side = source >> BITS[which] & 1
                    sides[place][side] = sides[place][side] + coef * phase
    for place in range(4):
        out = mine_ref if place < 2 else other_ref
        for side in range(2):
            value = sides[place][side] + jnp.where(is_upper == side, own_side[place], zero)
            out[place % 2, :, side * 128 : side * 128 + 128] = value


def per_device(scenes, date_pairs, first_weight, mid_weight, last_weight, inversion):
    groups = lax.axis_size("date")
    strips = lax.axis_size("strip")
    width = PIECE_COLS * LOOK_C
    rows = scenes.shape[2]
    ch = first_weight.shape[2]
    pairs = date_pairs.T

    piece = (2, rows, width)
    sends = pl.pallas_call(
        prep_kernel,
        name="prep",
        out_shape=[pltpu.VMEM(piece, BF)] * 3,
        in_specs=[spec(VMEM), spec(pl.ANY)],
        out_specs=[spec(VMEM)] * 3,
        scratch_shapes=[pltpu.SemaphoreType.DMA((3,))],
    )(pairs, scenes)
    *owns, signs = pl.pallas_call(
        own_kernel,
        name="own",
        out_shape=[pltpu.VMEM(piece, BF)] * 3 + [pltpu.VMEM((3, 8, 128), F32)],
        in_specs=[spec(VMEM), spec(pl.ANY)],
        out_specs=[spec(VMEM)] * 4,
        scratch_shapes=[pltpu.SemaphoreType.DMA((3,))],
    )(pairs, scenes)

    recvs = {}
    for slot, which in enumerate(SWAPS):
        route = [(low, low ^ 1 << BITS[which]) for low in range(groups)]
        recvs[which] = lax.ppermute(sends[slot], "date", route)

    coef = pl.pallas_call(
        coef_kernel,
        name="coef",
        out_shape=pltpu.SMEM((12 * groups,), F32),
        in_specs=[spec(SMEM), spec(SMEM)],
        out_specs=spec(SMEM),
        cost_estimate=pl.CostEstimate(flops=2000000, bytes_accessed=4000000, transcendentals=0),
    )(pairs, inversion.T)

    w1 = jnp.transpose(first_weight, (2, 0, 1, 3)).reshape(ch, 9, 2)
    w1 = jnp.stack(
        [jnp.pad(w1, ((0, 0), (0, 0), (2 * m, 6 - 2 * m))).reshape(ch, 72) for m in range(2)]
    )
    w2 = jnp.transpose(mid_weight, (0, 1, 3, 2, 4)).reshape(2, 3 * ch, 3 * ch)
    w4 = jnp.transpose(last_weight[:, :, 0], (1, 0, 2))
    w4 = jnp.pad(w4, ((0, 0), (0, 5), (0, 0))).reshape(24, ch)

    def looked_of(matchings):
        count = len(matchings)
        looked = pl.pallas_call(
            functools.partial(coherence_kernel, matchings),
            out_shape=pltpu.VMEM((8, FLAT), BF),
            in_specs=[spec(VMEM)] * (1 + 2 * count),
            out_specs=spec(VMEM),
            scratch_shapes=[pltpu.VMEM((8, FLAT), F32)],
        )(
            in_vmem(signs),
            *[in_vmem(recvs[which]) for which in matchings],
            *[in_vmem(owns[which]) for which in matchings],
        )
        up = lax.ppermute(looked, "strip", [(i, (i + 1) % strips) for i in range(strips)])
        down = lax.ppermute(looked, "strip", [((i + 1) % strips, i) for i in range(strips)])
        return looked, up, down

    def phases_of(matchings, looked, shape, *more):
        return pl.pallas_call(
            functools.partial(conv_kernel, matchings),
            out_shape=pltpu.VMEM(shape, BF),
            in_specs=[spec(VMEM)] * (6 + len(more)),
            out_specs=spec(VMEM),
            scratch_shapes=[
                pltpu.VMEM((8, EXT), F32),
                pltpu.VMEM((72, EXT), BF),
                pltpu.VMEM((len(matchings), 2, ch, PART + 256), BF),
                pltpu.VMEM((len(matchings), 2, ch, PART + 256), BF),
                pltpu.VMEM((len(matchings), 2, 8, 768), F32),
                pltpu.VMEM((8, EXT), F32),
                pltpu.VMEM((len(matchings), 8, 128), F32),
            ],
        )(
            *[in_vmem(v) for v in looked], *[in_vmem(v) for v in (w1, w2, w4)],
            *[in_vmem(v) for v in more],
        )

    done = []
    looked = [looked_of(group) for group in GROUPS]
    for group, value in zip(GROUPS, looked):
        if group is not GROUPS[-1]:
            shape = (len(group), STRIP_ROWS, 128)
            done.append(phases_of(group, value, shape))
    by_matching = {group[0]: value for group, value in zip(GROUPS, done)}
    rest = [by_matching[which] for which in sorted(by_matching)]
    half = groups // 2
    shape = (half, 3, STRIP_ROWS, 128)
    phases = phases_of(GROUPS[-1], looked[-1], shape, *rest)

    halves = [list(range(half)), list(range(half, groups))]
    gathered = lax.all_to_all(phases, "date", 0, 0, tiled=True, axis_index_groups=halves)

    mine, other = pl.pallas_call(
        sum_kernel,
        name="sums",
        out_shape=[pltpu.VMEM((2, STRIP_ROWS, 256), F32)] * 2,
        in_specs=[spec(SMEM), spec(VMEM)],
        out_specs=[spec(VMEM)] * 2,
    )(pltpu.with_memory_space_constraint(coef, pltpu.SMEM), in_vmem(gathered))
    route = [(low, low ^ half) for low in range(groups)]
    return mine + lax.ppermute(other, "date", route)


def solution(mesh):
    return jax.shard_map(
        per_device,
        mesh=mesh,
        in_specs=(P(None, "date", "strip", None), P(), P(), P(), P(), P()),
        out_specs=P("date", "strip", None),
        check_vma=False,
    )
```
